32 devices in a mesh: rows: 8 (over y, x, core), tp: 4 (over z).
Axes of the slice: x: 2, y: 2, z: 4, core: 2. Of those that a mesh axis runs over, the one named last changes fastest.
Arguments:
- hidden: bfloat16 [2048, 8, 1024], P('tp', 'rows'), may hold values from -6 to 6
- cotangent: bfloat16 [2048, 8, 1024], P('tp', 'rows'), may hold values from -6 to 6
- pair_lengths: int32 [8, 12], P('rows'), may hold values from 1 to 512, 2048 in all within a row
- w_qkv: bfloat16 [3, 1024, 1024], P(None, 'rows', 'tp'), may hold values from -0.1875 to 0.1875
- qkv_bias: bfloat16 [3, 1024], P(None, 'tp'), may hold values from -3 to 3
- w_out: bfloat16 [1024, 1024], P('tp', 'rows'), may hold values from -1.5 to 1.5
- w_up: bfloat16 [1024, 4096], P('rows', 'tp'), may hold values from -0.1875 to 0.1875
- up_bias: bfloat16 [4096], P('tp'), may hold values from -3 to 3
- w_down: bfloat16 [4096, 1024], P('tp', 'rows'), may hold values from -0.09375 to 0.09375
- resid_bias: bfloat16 [2, 1024], replicated, may hold values from -3 to 3
- norm_gain: bfloat16 [2, 1024], replicated, may hold values from 0.5 to 1.5
- norm_bias: bfloat16 [2, 1024], replicated, may hold values from -2 to 2
- prefix_keys: bfloat16 [64, 1024], P(None, 'tp'), may hold values from -6 to 6
- prefix_values: bfloat16 [64, 1024], P(None, 'tp'), may hold values from -6 to 6
Outputs:
- result: bfloat16 [2048, 8, 1024], P('tp', 'rows')
- grad_input: float32 [2048, 8, 1024], P('tp', 'rows')
- key_total: float32 [64, 1024], P(None, 'tp')
- value_total: float32 [64, 1024], P(None, 'tp')
The draws below stay inside these ranges and needn't reach their ends.
Inputs may be any that keep to these rules, and one draw needn't show every extreme that they name: Each row of pair_lengths holds 11 pair lengths followed by the length of the trailing pad; a row's entries sum to 2048 and its largest is exactly 512.
All inputs are finite; a program needn't handle non-finite values.
Results may differ from the reference program's by a relative error of at most 0.015.
Values may be sent and summed in bfloat16 or wider, within the bound.
No kernel may reach another device: no remote copies, remote signals or barrier semaphores. Data moves between devices by JAX's collectives and lax.ppermute only.
A program may use at most 128 MiB of HBM per device.

```python
import math
import jax
import jax.numpy as jnp
import numpy as np
from jax import lax

D = 1024
HEADS = 16
HEAD_DIM = 64
FF = 4096
PREFIX = 64
SEQ = 2048
MAXLEN = 512
PAIRS = 11
QBLOCK = 512
ROWS = 8


def steps_of(key, shape, cuts, low, largest):
    factor_of = 1.0
    for axis_at, parts in cuts:
        heights = jax.random.uniform(jax.random.fold_in(jax.random.fold_in(key, 6), axis_at), (parts,), jnp.float32, low / len(cuts), largest / len(cuts))
        factor_of = factor_of * jnp.repeat(jnp.exp(heights), shape[axis_at] // parts).reshape((-1,) + (1,) * (len(shape) - 1 - axis_at))
    return factor_of


def length_profile(count, total, reach, slope):
    weights = [(1 << 20) // math.isqrt(grade ** slope) + 1 for grade in range(2, count + 1)]
    rest, given = total - reach - (count - 1), [1] * (count - 1)
    while rest > 0:
        free = [i for i in range(count - 1) if given[i] < reach]
        mass, left = sum([weights[i] for i in free]), rest
        for i in free:
            more = min(reach - given[i], max(1, left * weights[i] // mass), rest)
            given[i] = given[i] + more
            rest = rest - more
    return np.array([reach] + given)


def ragged(own_key, count, total, reach, skew):
    if count == 2:
        one = jax.random.randint(own_key, (), max(1, total - reach), min(reach, total - 1) + 1)
        return jnp.stack([one, total - one])
    tallies = jnp.asarray(length_profile(count, total, reach, skew), jnp.int32)
    couples = (count - 1) // 2
    donor, receiver = tallies[1:1 + 2 * couples:2], tallies[2:2 + 2 * couples:2]
    slack = jnp.minimum(donor - 1, reach - receiver)
    moved = jax.random.randint(jax.random.fold_in(own_key, 1), (couples,), 0, 1 << 20) % (slack + 1)
    tallies = tallies.at[1:1 + 2 * couples:2].set(donor - moved).at[2:2 + 2 * couples:2].set(receiver + moved)
    return tallies[jax.random.permutation(jax.random.fold_in(own_key, 2), count)]


def normal_values(own_key, shape, deviation, bound, cuts=(), held_as=jnp.bfloat16):
    level = steps_of(own_key, shape, cuts, -0.22, 0.18) if cuts else 1.0
    drawn = jax.random.normal(own_key, shape, jnp.float32) * deviation * level
    return jnp.minimum(jnp.maximum(drawn, -bound), bound).astype(held_as)


def setup_inputs(seed: int = 0) -> dict:
    splits = jax.random.split(jax.random.key(seed), 15)
    hidden = normal_values(splits[0], (SEQ, ROWS, D), 1.0, 6.0, ((0, 4), (1, 8)))
    cotangent = normal_values(splits[1], (SEQ, ROWS, D), 1.0, 6.0, ((0, 4), (1, 8)))
    pair_lengths = jax.vmap(lambda own: ragged(own, PAIRS + 1, SEQ, MAXLEN, 2))(jax.random.split(splits[2], ROWS)).reshape((ROWS, PAIRS + 1)).astype(jnp.int32)
    w_qkv = normal_values(splits[3], (3, D, D), D ** -0.5, 0.1875, ((1, 8), (2, 4)))
    qkv_bias = normal_values(splits[4], (3, D), 0.5, 3.0, ((1, 4),))
    w_out = normal_values(splits[5], (D, D), (D // 64) ** -0.5, 1.5, ((0, 4), (1, 8)))
    w_up = normal_values(splits[6], (D, FF), D ** -0.5, 0.1875, ((0, 8), (1, 4)))
    up_bias = normal_values(splits[7], (FF,), 0.5, 3.0, ((0, 4),))
    w_down = normal_values(splits[8], (FF, D), FF ** -0.5, 0.09375, ((0, 4), (1, 8)))
    resid_bias = normal_values(splits[9], (2, D), 0.5, 3.0)
    norm_gain = jnp.clip(1.0 + 0.1 * jax.random.normal(splits[10], (2, D), jnp.float32), 0.5, 1.5).astype(jnp.bfloat16)
    norm_bias = normal_values(splits[11], (2, D), 0.3, 2.0)
    prefix_keys = normal_values(splits[12], (PREFIX, D), 1.0, 6.0, ((1, 4),))
    prefix_values = normal_values(splits[13], (PREFIX, D), 1.0, 6.0, ((1, 4),))
    return {"hidden": hidden, "cotangent": cotangent, "pair_lengths": pair_lengths, "w_qkv": w_qkv, "qkv_bias": qkv_bias, "w_out": w_out, "w_up": w_up, "up_bias": up_bias, "w_down": w_down, "resid_bias": resid_bias, "norm_gain": norm_gain, "norm_bias": norm_bias, "prefix_keys": prefix_keys, "prefix_values": prefix_values}


@jax.custom_vjp
def low(v):
    return lax.optimization_barrier(v.astype(jnp.bfloat16)).astype(jnp.float32)

@jax.custom_vjp
def low_back(v):
    return v

def low_keep(v):
    return (low(v), None)

def low_pass(kept, grad):
    return (grad,)

def back_keep(v):
    return (v, None)

def back_low(kept, grad):
    return (low(grad),)
low.defvjp(low_keep, low_pass)
low_back.defvjp(back_keep, back_low)
EPS = 1e-05
NEG = -1e+30
HIGH = lax.Precision.HIGHEST

def rounded_both(values):
    return low(low_back(values))

def layer_norm(values, gain, shift):
    mean = lax.optimization_barrier(jnp.mean(values, axis=-1, keepdims=True))
    centred = values - mean
    variance = lax.optimization_barrier(jnp.mean(centred * centred, axis=-1, keepdims=True))
    return centred * lax.rsqrt(variance + EPS) * gain + shift

def segment_row(lengths_row):
    ends = jnp.cumsum(lengths_row)
    place = jnp.arange(SEQ, dtype=jnp.int32)
    return lax.optimization_barrier(jnp.sum((place[:, None] >= ends[None, :]).astype(jnp.int32), axis=1))

def row_forward(hidden_row, lengths_row, weights, key_prefix, value_prefix):
    w_qkv, qkv_bias, w_out, w_up, up_bias, w_down, resid_bias, norm_gain, norm_bias = weights
    scale = HEAD_DIM ** (-0.5)
    seg_row = segment_row(lengths_row)
    pad_id = lengths_row.shape[0] - 1
    packed = jnp.einsum('sd,jde->jse', hidden_row, w_qkv, precision=HIGH) + qkv_bias[:, None, :]
    packed = rounded_both(packed)
    queries = packed[0].reshape(SEQ // QBLOCK, QBLOCK, HEADS, HEAD_DIM)
    keys_all = jnp.concatenate([key_prefix, packed[1]], axis=0).reshape(PREFIX + SEQ, HEADS, HEAD_DIM)
    values_all = jnp.concatenate([value_prefix, packed[2]], axis=0).reshape(PREFIX + SEQ, HEADS, HEAD_DIM)
    key_seg = jnp.concatenate([jnp.full((PREFIX,), -1, jnp.int32), seg_row])
    is_prefix = jnp.arange(PREFIX + SEQ, dtype=jnp.int32) < PREFIX

    def block(args):
        query_block, seg_block = args
        scores = jnp.einsum('qhd,khd->hqk', query_block, keys_all, precision=HIGH) * scale
        allowed = is_prefix[None, :] | (key_seg[None, :] == seg_block[:, None]) & (seg_block[:, None] != pad_id)
        scores = low_back(jnp.where(allowed[None], scores, NEG))
        peak = lax.optimization_barrier(jnp.max(scores, axis=-1, keepdims=True))
        expo = jnp.exp(scores - peak)
        probs = expo / lax.optimization_barrier(jnp.sum(expo, axis=-1, keepdims=True))
        return jnp.einsum('hqk,khd->qhd', low(probs), values_all, precision=HIGH)
    mixed = lax.map(jax.checkpoint(block), (queries, seg_row.reshape(SEQ // QBLOCK, QBLOCK)))
    mixed = rounded_both(mixed.reshape(SEQ, D))
    attended = low_back(jnp.dot(mixed, w_out, precision=HIGH))
    first = hidden_row + attended + resid_bias[0]
    normed = layer_norm(first, norm_gain[0], norm_bias[0])
    expanded = low_back(jnp.dot(low(normed), w_up, precision=HIGH) + up_bias)
    active = low(jax.nn.gelu(expanded, approximate=False))
    lowered = low_back(jnp.dot(active, w_down, precision=HIGH))
    second = normed + lowered + resid_bias[1]
    return layer_norm(second, norm_gain[1], norm_bias[1])

def reference(hidden, cotangent, pair_lengths, w_qkv, qkv_bias, w_out, w_up, up_bias, w_down, resid_bias, norm_gain, norm_bias, prefix_keys, prefix_values):
    weights = tuple((value.astype(jnp.float32) for value in (w_qkv, qkv_bias, w_out, w_up, up_bias, w_down, resid_bias, norm_gain, norm_bias)))
    rows_in = jnp.moveaxis(hidden.astype(jnp.float32), 1, 0)
    rows_cot = jnp.moveaxis(cotangent.astype(jnp.float32), 1, 0)

    def forward(inputs, key_prefix, value_prefix):

        def one(args):
            return row_forward(args[0], args[1], weights, key_prefix, value_prefix)
        return lax.map(jax.checkpoint(one), (inputs, pair_lengths))
    result, pull = jax.vjp(forward, rows_in, prefix_keys.astype(jnp.float32), prefix_values.astype(jnp.float32))
    grad_rows, key_total, value_total = pull(rows_cot)
    return (jnp.moveaxis(result, 0, 1).astype(jnp.bfloat16), jnp.moveaxis(grad_rows, 0, 1), key_total, value_total)
```

```python
from functools import partial

import jax
import jax.numpy as jnp
from jax import lax
from jax.experimental import pallas as pl
from jax.experimental.pallas import tpu as pltpu
from jax.sharding import PartitionSpec as P

HEAD_DIM = 64
PREFIX = 64
SEQ = 2048
MAXLEN = 512
EPS = 1e-05
NEG = -1e30
BLOCK = 256
LANES = 128
F32 = jnp.float32
BF16 = jnp.bfloat16


def layer_norm(values, gain, shift):
    mean = jnp.mean(values, axis=-1, keepdims=True)
    centred = values - mean
    variance = jnp.mean(centred * centred, axis=-1, keepdims=True)
    return centred * lax.rsqrt(variance + EPS) * gain + shift


def norm_back(values, gain, shift, grad):
    unused, pull = jax.vjp(lambda inner: layer_norm(inner, gain, shift), values)
    return pull(grad)[0]


def dot(a, b):
    return jnp.dot(a, b, preferred_element_type=F32)


def dot_t(a, b):
    return lax.dot_general(a, b, (((1,), (1,)), ((), ())), preferred_element_type=F32)


def halves(x):
    lane = lax.broadcasted_iota(jnp.int32, x.shape, 1)
    zero = jnp.zeros_like(x)
    return (jnp.where(lane < HEAD_DIM, x, zero), jnp.where(lane < HEAD_DIM, zero, x))


def key_mask(kb, shape, start, end):
    at = lax.broadcasted_iota(jnp.int32, shape, 0) + kb * BLOCK
    return (at >= start) & (at < end)


def attend_kernel(lo_ref, hi_ref, q_ref, k_ref, v_ref, kp_ref, vp_ref, b_ref, o_ref, l_ref, vt_ref):
    tokens, lanes = q_ref.shape
    window = k_ref.shape[0]
    step = min(BLOCK, tokens)
    pairs = lanes // LANES
    for p in range(pairs):
        for i in range(window // BLOCK):
            vt_ref[p, i] = v_ref[i * BLOCK : (i + 1) * BLOCK, p * LANES : (p + 1) * LANES].T
    for qb in range(tokens // step):
        rows = slice(qb * step, (qb + 1) * step)
        start = b_ref[0:1, rows]
        end = b_ref[1:2, rows]
        queries = []
        carry = []
        for p in range(pairs):
            cols = slice(p * LANES, (p + 1) * LANES)
            queries += halves(q_ref[rows, cols] * 0.125)
            vpt = vp_ref[:, cols].T
            for h in range(2):
                s = dot_t(kp_ref[:, cols], queries[2 * p + h])
                m = jnp.max(s, axis=0, keepdims=True)
                e = jnp.exp(s - m)
                carry += [
                    m,
                    jnp.sum(e, axis=0, keepdims=True),
                    dot(vpt[h * HEAD_DIM : (h + 1) * HEAD_DIM], e.astype(BF16)),
                ]

        def body(kb, carry):
            mask = key_mask(kb, (BLOCK, step), start, end)
            out = []
            at = pl.multiple_of(kb * BLOCK, BLOCK)
            for p in range(pairs):
                keys = k_ref[pl.ds(at, BLOCK), p * LANES : (p + 1) * LANES]
                vt = vt_ref[p, kb]
                for h in range(2):
                    m, total, acc = carry[3 * (2 * p + h) : 3 * (2 * p + h) + 3]
                    s = jnp.where(mask, dot_t(keys, queries[2 * p + h]), NEG)
                    top = jnp.maximum(m, jnp.max(s, axis=0, keepdims=True))
                    alpha = jnp.exp(m - top)
                    e = jnp.exp(s - top)
                    out += [
                        top,
                        total * alpha + jnp.sum(e, axis=0, keepdims=True),
                        acc * alpha + dot(vt[h * HEAD_DIM : (h + 1) * HEAD_DIM], e.astype(BF16)),
                    ]
            return tuple(out)

        carry = lax.fori_loop(lo_ref[qb], hi_ref[qb], body, tuple(carry))
        for p in range(pairs):
            both = []
            for h in range(2):
                m, total, acc = carry[3 * (2 * p + h) : 3 * (2 * p + h) + 3]
                both.append(acc / total)
                l_ref[0, 2 * p + h : 2 * p + h + 1, rows] = m + jnp.log(total)
            o_ref[rows, p * LANES : (p + 1) * LANES] = jnp.concatenate(both, axis=0).T.astype(BF16)


def attend_back_kernel(
    lo_ref, hi_ref, q_ref, k_ref, v_ref, kp_ref, vp_ref, b_ref, o_ref, l_ref, do_ref,
    dq_ref, dk_ref, dv_ref, dkp_ref, dvp_ref, kt_ref, ka_ref, va_ref,
):
    tokens, lanes = q_ref.shape
    window = k_ref.shape[0]
    step = min(BLOCK, tokens)
    pairs = lanes // LANES
    for p in range(pairs):
        for i in range(window // BLOCK):
            kt_ref[p, i] = k_ref[i * BLOCK : (i + 1) * BLOCK, p * LANES : (p + 1) * LANES].T
    ka_ref[...] = jnp.zeros(ka_ref.shape, F32)
    va_ref[...] = jnp.zeros(va_ref.shape, F32)
    for qb in range(tokens // step):
        rows = slice(qb * step, (qb + 1) * step)
        start = b_ref[0:1, rows]
        end = b_ref[1:2, rows]
        queries, grads, sums, inner, joint_q, joint_g, carry = [], [], [], [], [], [], []

        def pieces(keys, values, p, mask):
            prob, dsc = [], []
            for h in range(2):
                n = 2 * p + h
                s = dot_t(keys, queries[n])
                if mask is not None:
                    s = jnp.where(mask, s, NEG)
                e = jnp.exp(s - sums[n])
                d = e * (dot_t(values, grads[n]) - inner[n])
                prob.append(e.astype(BF16))
                dsc.append(d.astype(BF16))
            dk = dot(jnp.concatenate(dsc, axis=1), joint_q[p])
            dv = dot(jnp.concatenate(prob, axis=1), joint_g[p])
            return dsc, dk, dv

        for p in range(pairs):
            cols = slice(p * LANES, (p + 1) * LANES)
            queries += halves(q_ref[rows, cols] * 0.125)
            grads += halves(do_ref[rows, cols])
            joint_q.append(jnp.concatenate(queries[2 * p :], axis=0))
            joint_g.append(jnp.concatenate(grads[2 * p :], axis=0))
            prod = (do_ref[rows, cols].astype(F32) * o_ref[rows, cols].astype(F32)).T
            for h in range(2):
                inner.append(jnp.sum(prod[h * HEAD_DIM : (h + 1) * HEAD_DIM], axis=0, keepdims=True))
                sums.append(l_ref[0, 2 * p + h : 2 * p + h + 1, rows])
            keys = kp_ref[:, cols]
            dsc, dk, dv = pieces(keys, vp_ref[:, cols], p, None)
            if qb == 0:
                dkp_ref[:, cols] = dk
                dvp_ref[:, cols] = dv
            else:
                dkp_ref[:, cols] += dk
                dvp_ref[:, cols] += dv
            kpt = keys.T
            for h in range(2):
                carry.append(dot(kpt[h * HEAD_DIM : (h + 1) * HEAD_DIM], dsc[h]))

        def body(kb, carry):
            mask = key_mask(kb, (BLOCK, step), start, end)
            out = []
            at = pl.multiple_of(kb * BLOCK, BLOCK)
            for p in range(pairs):
                cols = slice(p * LANES, (p + 1) * LANES)
                keys = k_ref[pl.ds(at, BLOCK), cols]
                dsc, dk, dv = pieces(keys, v_ref[pl.ds(at, BLOCK), cols], p, mask)
                ka_ref[pl.ds(at, BLOCK), cols] += dk
                va_ref[pl.ds(at, BLOCK), cols] += dv
                kt = kt_ref[p, kb]
                for h in range(2):
                    out.append(
                        carry[2 * p + h] + dot(kt[h * HEAD_DIM : (h + 1) * HEAD_DIM], dsc[h])
                    )
            return tuple(out)

        carry = lax.fori_loop(lo_ref[qb], hi_ref[qb], body, tuple(carry))
        for p in range(pairs):
            both = jnp.concatenate(carry[2 * p : 2 * p + 2], axis=0)
            dq_ref[rows, p * LANES : (p + 1) * LANES] = (both.T * 0.125).astype(BF16)
    dk_ref[...] = ka_ref[...].astype(BF16)
    dv_ref[...] = va_ref[...].astype(BF16)


def specs(tokens, window, lanes, per):
    col = lambda i, *s: (0, i)
    return dict(
        tok=pl.BlockSpec((tokens, lanes), col),
        win=pl.BlockSpec((window, lanes), col),
        pre=pl.BlockSpec((PREFIX, lanes), col),
        bnd=pl.BlockSpec((8, tokens), lambda i, *s: (0, 0)),
        lse=pl.BlockSpec((1, per, tokens), lambda i, *s: (i, 0, 0)),
    )


def attend(lo, hi, q, k, v, kp, vp, bounds, lanes):
    tokens, width = q.shape
    window = k.shape[0]
    per = lanes // HEAD_DIM
    s = specs(tokens, window, lanes, per)
    return pl.pallas_call(
        attend_kernel,
        grid_spec=pltpu.PrefetchScalarGridSpec(
            num_scalar_prefetch=2,
            grid=(width // lanes,),
            in_specs=[s["tok"], s["win"], s["win"], s["pre"], s["pre"], s["bnd"]],
            out_specs=[s["tok"], s["lse"]],
            scratch_shapes=[pltpu.VMEM((lanes // LANES, window // BLOCK, LANES, BLOCK), BF16)],
        ),
        out_shape=[
            jax.ShapeDtypeStruct((tokens, width), BF16),
            jax.ShapeDtypeStruct((width // lanes, per, tokens), F32),
        ],
        name="attend",
    )(lo, hi, q, k, v, kp, vp, bounds)


def attend_back(lo, hi, q, k, v, kp, vp, bounds, o, lse, do, lanes):
    tokens, width = q.shape
    window = k.shape[0]
    s = specs(tokens, window, lanes, lanes // HEAD_DIM)
    return pl.pallas_call(
        attend_back_kernel,
        grid_spec=pltpu.PrefetchScalarGridSpec(
            num_scalar_prefetch=2,
            grid=(width // lanes,),
            in_specs=[
                s["tok"], s["win"], s["win"], s["pre"], s["pre"], s["bnd"],
                s["tok"], s["lse"], s["tok"],
            ],
            out_specs=[s["tok"], s["win"], s["win"], s["pre"], s["pre"]],
            scratch_shapes=[
                pltpu.VMEM((lanes // LANES, window // BLOCK, LANES, BLOCK), BF16),
                pltpu.VMEM((window, lanes), F32),
                pltpu.VMEM((window, lanes), F32),
            ],
        ),
        out_shape=[
            jax.ShapeDtypeStruct((tokens, width), BF16),
            jax.ShapeDtypeStruct((window, width), BF16),
            jax.ShapeDtypeStruct((window, width), BF16),
            jax.ShapeDtypeStruct((PREFIX, width), F32),
            jax.ShapeDtypeStruct((PREFIX, width), F32),
        ],
        name="attend_back",
    )(lo, hi, q, k, v, kp, vp, bounds, o, lse, do)


def swap(x, axis, bit, size):
    return lax.ppermute(x, axis, [(i, i ^ (1 << bit)) for i in range(size)])


def join(mine, theirs, axis, inner):
    count = mine.shape[axis] // inner
    parts = []
    for c in range(count):
        for side in (mine, theirs):
            parts.append(lax.slice_in_dim(side, c * inner, (c + 1) * inner, axis=axis))
    return jnp.concatenate(parts, axis=axis)


def bits_of(size):
    count = size.bit_length() - 1
    assert 1 << count == size
    return count


def gather(w, order, d_axis, rows, tp):
    block = w.shape[d_axis]
    have = set()
    for kind, bit in order:
        if kind == "tp":
            w = join(w, swap(w, "tp", bit, tp), 1 - d_axis, w.shape[1 - d_axis])
        else:
            inner = w.shape[d_axis]
            if bit:
                inner = block * (1 << len([b for b in have if 0 < b < bit]))
            w = join(w, swap(w, "rows", bit, rows), d_axis, inner)
            have.add(bit)
    return w


def orders(rows, tp):
    zs = [("tp", b) for b in reversed(range(bits_of(tp)))]
    rs = [("rows", b) for b in range(1, bits_of(rows))]
    core = [("rows", 0)]
    half = len(rs) // 2
    return (
        zs[:-1] + rs + zs[-1:] + core,
        zs + rs + core,
        zs[:-1] + rs[half:] + zs[-1:] + rs[:half] + core,
    )


def reorder_kernel(at_ref, *refs):
    half = len(refs) // 2
    for a, b in zip(refs[:half], refs[half:]):
        b[...] = a[...]


def reorder(place, arrays):
    count = place.shape[0]
    width = arrays[0].shape[1]
    block = width // count
    if block % LANES:
        return [
            jnp.take(a.reshape(a.shape[0], count, block), place, axis=1).reshape(a.shape)
            for a in arrays
        ]
    return pl.pallas_call(
        reorder_kernel,
        grid_spec=pltpu.PrefetchScalarGridSpec(
            num_scalar_prefetch=1,
            grid=(count,),
            in_specs=[pl.BlockSpec((a.shape[0], block), lambda i, at: (0, at[i])) for a in arrays],
            out_specs=[pl.BlockSpec((a.shape[0], block), lambda i, at: (0, i)) for a in arrays],
        ),
        out_shape=[jax.ShapeDtypeStruct(a.shape, a.dtype) for a in arrays],
        name="reorder",
    )(place, *arrays)


def shift(x, step, tp):
    return lax.ppermute(x, "tp", [(i, i + step) for i in range(tp) if 0 <= i + step < tp])


def body(
    rows, tp,
    hidden, cotangent, pair_lengths, w_qkv, qkv_bias, w_out, w_up, up_bias, w_down,
    resid_bias, norm_gain, norm_bias, prefix_keys, prefix_values,
):
    tokens, row_count, width = hidden.shape
    assert row_count == 1
    local = w_qkv.shape[2]
    hops = -(-(MAXLEN - 1) // tokens)
    halo = hops * tokens
    window = tokens + 2 * halo
    lanes = min(width, 2 * LANES)
    here = lax.axis_index("tp")
    row = lax.axis_index("rows")
    order_a, order_b, order_c = orders(rows, tp)
    z_order = [o for o in order_b if o[0] == "tp"]
    nr = bits_of(rows)
    masks = [((s & ((rows >> 1) - 1)) << 1) | (s >> (nr - 1)) for s in range(rows)]
    place = (row ^ jnp.array(masks, jnp.int32)).astype(jnp.int32)

    hid, cot, shifts, gains, offsets = reorder(
        place, [hidden[:, 0], cotangent[:, 0], resid_bias, norm_gain, norm_bias]
    )
    shifts, gains, offsets = (a.astype(F32) for a in (shifts, gains, offsets))
    hid_window = jnp.concatenate(
        [shift(hid, j, tp) for j in range(hops, 0, -1)]
        + [hid]
        + [shift(hid, -j, tp) for j in range(1, hops + 1)],
        axis=0,
    )

    packed_small = jnp.concatenate(
        [prefix_keys, prefix_values, qkv_bias, up_bias.reshape(-1, local)], axis=0
    )
    small = gather(packed_small, z_order, 0, rows, tp)
    key_prefix, value_prefix = small[:PREFIX], small[PREFIX : 2 * PREFIX]
    biases = small[2 * PREFIX : 2 * PREFIX + 3].astype(F32)
    up_shift = (
        small[2 * PREFIX + 3 :].reshape(-1, tp, local).swapaxes(0, 1).reshape(-1).astype(F32)
    )

    wq = gather(w_qkv[0], order_c, 0, rows, tp)
    wk = gather(w_qkv[1], order_a, 0, rows, tp)
    wv = gather(w_qkv[2], order_b, 0, rows, tp)
    out_full = gather(w_out, order_c, 1, rows, tp)
    ff = w_up.shape[1] // 2
    up_full = [
        gather(w_up[:, :ff], order_a, 0, rows, tp),
        gather(w_up[:, ff:], order_b, 0, rows, tp),
    ]
    down_full = [
        gather(w_down[:ff], order_c, 1, rows, tp),
        gather(w_down[ff:], order_a, 1, rows, tp),
    ]
    up_shift = up_shift.reshape(tp, 2, ff)
    up_shifts = [up_shift[:, i].reshape(-1) for i in range(2)]

    ends = jnp.cumsum(pair_lengths[0])
    pad_id = ends.shape[0] - 1
    spot = here * tokens + jnp.arange(tokens, dtype=jnp.int32)
    past = spot[None, :] >= ends[:, None]
    seg = jnp.sum(past.astype(jnp.int32), axis=0)
    base = here * tokens - halo
    live = seg != pad_id
    first_key = jnp.max(jnp.where(past, ends[:, None], 0), axis=0) - base
    last_key = jnp.min(jnp.where(past, SEQ, ends[:, None]), axis=0) - base
    step = min(BLOCK, tokens)
    lo = jnp.min(jnp.where(live, first_key, window).reshape(-1, step), axis=1)
    hi = jnp.max(jnp.where(live, last_key, 0).reshape(-1, step), axis=1)
    lo = lo // BLOCK
    hi = jnp.maximum((hi + BLOCK - 1) // BLOCK, lo)
    zero = jnp.zeros_like(first_key)
    bounds = jnp.stack(
        [jnp.where(live, first_key, 0), jnp.where(live, last_key, 0)] + [zero] * 6, axis=0
    )

    q = (dot(hid, wq) + biases[0]).astype(BF16)
    k = (dot(hid_window, wk) + biases[1]).astype(BF16)
    v = (dot(hid_window, wv) + biases[2]).astype(BF16)
    mixed, lse = attend(lo, hi, q, k, v, key_prefix, value_prefix, bounds, lanes)
    first = hid.astype(F32) + dot(mixed, out_full) + shifts[0]
    normed = layer_norm(first, gains[0], offsets[0])
    normed_low = normed.astype(BF16)
    expanded = [dot(normed_low, w) + b for w, b in zip(up_full, up_shifts)]
    active = [jax.nn.gelu(e, approximate=False).astype(BF16) for e in expanded]
    second = normed + (dot(active[0], down_full[0]) + dot(active[1], down_full[1])) + shifts[1]
    result = layer_norm(second, gains[1], offsets[1]).astype(BF16)

    grad_second = norm_back(second, gains[1], offsets[1], cot.astype(F32))
    grad_low = grad_second.astype(BF16)
    grad_normed = grad_second
    for i in range(2):
        unused, pull = jax.vjp(partial(jax.nn.gelu, approximate=False), expanded[i])
        grad_hidden = pull(dot_t(grad_low, down_full[i]))[0].astype(BF16)
        grad_normed = grad_normed + dot_t(grad_hidden, up_full[i])
    grad_first = norm_back(first, gains[0], offsets[0], grad_normed)
    grad_mixed = dot_t(grad_first.astype(BF16), out_full).astype(BF16)
    dq, dk, dv, dkp, dvp = attend_back(
        lo, hi, q, k, v, key_prefix, value_prefix, bounds, mixed, lse, grad_mixed, lanes
    )

    grad_kv = dot_t(dk, wk) + dot_t(dv, wv)
    grad_input = grad_kv[halo : halo + tokens] + dot_t(dq, wq) + grad_first
    for j in range(1, hops + 1):
        below = grad_kv[halo - j * tokens : halo - (j - 1) * tokens].astype(BF16)
        above = grad_kv[halo + j * tokens : halo + (j + 1) * tokens].astype(BF16)
        grad_input = grad_input + shift(below, -j, tp).astype(F32)
        grad_input = grad_input + shift(above, j, tp).astype(F32)

    total = jnp.concatenate([dkp, dvp], axis=0)
    for kind, bit in reversed(z_order):
        half = total.shape[1] // 2
        total = total[:, :half] + swap(total[:, half:], "tp", bit, tp)
    for bit in range(nr):
        total = total + swap(total, "rows", bit, rows)

    apart = (row ^ jnp.arange(rows, dtype=jnp.int32)).astype(jnp.int32)
    back = (apart >> 1) | ((apart & 1) << (nr - 1))
    result, grad_input = reorder(back, [result, grad_input])
    return result[:, None], grad_input[:, None], total[:PREFIX], total[PREFIX:]


def solution(mesh):
    placed = (
        P("tp", "rows", None),
        P("tp", "rows", None),
        P("rows", None),
        P(None, "rows", "tp"),
        P(None, "tp"),
        P("tp", "rows"),
        P("rows", "tp"),
        P("tp"),
        P("tp", "rows"),
        P(),
        P(),
        P(),
        P(None, "tp"),
        P(None, "tp"),
    )
    return jax.shard_map(
        partial(body, mesh.shape["rows"], mesh.shape["tp"]),
        mesh=mesh,
        in_specs=placed,
        out_specs=(P("tp", "rows", None), P("tp", "rows", None), P(None, "tp"), P(None, "tp")),
        check_vma=False,
    )
```

```python
from functools import partial

import jax
import jax.numpy as jnp
from jax import lax
from jax.experimental import pallas as pl
from jax.experimental.pallas import tpu as pltpu
from jax.sharding import PartitionSpec as P

HEAD_DIM = 64
PREFIX = 64
SEQ = 2048
MAXLEN = 512
EPS = 1e-05
NEG = -1e30
EARLY = 3
BLOCK = 256
FFBLOCK = 512
LANES = 128
F32 = jnp.float32
BF16 = jnp.bfloat16


def layer_norm(values, gain, shift):
    mean = jnp.mean(values, axis=-1, keepdims=True)
    centred = values - mean
    variance = jnp.mean(centred * centred, axis=-1, keepdims=True)
    return centred * lax.rsqrt(variance + EPS) * gain + shift


def norm_back(values, gain, shift, grad):
    unused, pull = jax.vjp(lambda inner: layer_norm(inner, gain, shift), values)
    return pull(grad)[0]


def dot(a, b):
    return jnp.dot(a, b, preferred_element_type=F32)


def dot_t(a, b):
    return lax.dot_general(a, b, (((1,), (1,)), ((), ())), preferred_element_type=F32)


def halves(x):
    lane = lax.broadcasted_iota(jnp.int32, x.shape, 1)
    zero = jnp.zeros_like(x)
    return (jnp.where(lane < HEAD_DIM, x, zero), jnp.where(lane < HEAD_DIM, zero, x))


def key_mask(kb, shape, start, end):
    at = lax.broadcasted_iota(jnp.int32, shape, 0) + kb * BLOCK
    return (at >= start) & (at < end)


def attend_kernel(lo_ref, hi_ref, q_ref, k_ref, v_ref, kp_ref, vp_ref, b_ref, o_ref, l_ref, vt_ref):
    tokens, lanes = q_ref.shape
    window = k_ref.shape[0]
    step = min(BLOCK, tokens)
    pairs = lanes // LANES
    for p in range(pairs):
        for i in range(window // BLOCK):
            vt_ref[p, i] = v_ref[i * BLOCK : (i + 1) * BLOCK, p * LANES : (p + 1) * LANES].T
    for qb in range(tokens // step):
        rows = slice(qb * step, (qb + 1) * step)
        start = b_ref[0:1, rows]
        end = b_ref[1:2, rows]
        queries = []
        carry = []
        for p in range(pairs):
            cols = slice(p * LANES, (p + 1) * LANES)
            queries += halves(q_ref[rows, cols] * 0.125)
            vpt = vp_ref[:, cols].T
            for h in range(2):
                s = dot_t(kp_ref[:, cols], queries[2 * p + h])
                m = jnp.max(s, axis=0, keepdims=True)
                e = jnp.exp(s - m)
                carry += [
                    m,
                    jnp.sum(e, axis=0, keepdims=True),
                    dot(vpt[h * HEAD_DIM : (h + 1) * HEAD_DIM], e.astype(BF16)),
                ]

        def body(kb, carry):
            mask = key_mask(kb, (BLOCK, step), start, end)
            out = []
            at = pl.multiple_of(kb * BLOCK, BLOCK)
            for p in range(pairs):
                keys = k_ref[pl.ds(at, BLOCK), p * LANES : (p + 1) * LANES]
                vt = vt_ref[p, kb]
                for h in range(2):
                    m, total, acc = carry[3 * (2 * p + h) : 3 * (2 * p + h) + 3]
                    s = jnp.where(mask, dot_t(keys, queries[2 * p + h]), NEG)
                    top = jnp.maximum(m, jnp.max(s, axis=0, keepdims=True))
                    alpha = jnp.exp(m - top)
                    e = jnp.exp(s - top)
                    out += [
                        top,
                        total * alpha + jnp.sum(e, axis=0, keepdims=True),
                        acc * alpha + dot(vt[h * HEAD_DIM : (h + 1) * HEAD_DIM], e.astype(BF16)),
                    ]
            return tuple(out)

        carry = lax.fori_loop(lo_ref[qb], hi_ref[qb], body, tuple(carry))
        for p in range(pairs):
            both = []
            for h in range(2):
                m, total, acc = carry[3 * (2 * p + h) : 3 * (2 * p + h) + 3]
                both.append(acc / total)
                l_ref[0, 2 * p + h : 2 * p + h + 1, rows] = m + jnp.log(total)
            o_ref[rows, p * LANES : (p + 1) * LANES] = jnp.concatenate(both, axis=0).T.astype(BF16)


def attend_back_kernel(
    lo_ref, hi_ref, q_ref, k_ref, v_ref, kp_ref, vp_ref, b_ref, o_ref, l_ref, do_ref,
    dq_ref, dk_ref, dv_ref, dkp_ref, dvp_ref, kt_ref, ka_ref, va_ref,
):
    tokens, lanes = q_ref.shape
    window = k_ref.shape[0]
    step = min(BLOCK, tokens)
    pairs = lanes // LANES
    for p in range(pairs):
        for i in range(window // BLOCK):
            kt_ref[p, i] = k_ref[i * BLOCK : (i + 1) * BLOCK, p * LANES : (p + 1) * LANES].T
    ka_ref[...] = jnp.zeros(ka_ref.shape, F32)
    va_ref[...] = jnp.zeros(va_ref.shape, F32)
    for qb in range(tokens // step):
        rows = slice(qb * step, (qb + 1) * step)
        start = b_ref[0:1, rows]
        end = b_ref[1:2, rows]
        queries, grads, sums, inner, joint_q, joint_g, carry = [], [], [], [], [], [], []

        def pieces(keys, values, p, mask):
            prob, dsc = [], []
            for h in range(2):
                n = 2 * p + h
                s = dot_t(keys, queries[n])
                if mask is not None:
                    s = jnp.where(mask, s, NEG)
                e = jnp.exp(s - sums[n])
                d = e * (dot_t(values, grads[n]) - inner[n])
                prob.append(e.astype(BF16))
                dsc.append(d.astype(BF16))
            dk = dot(jnp.concatenate(dsc, axis=1), joint_q[p])
            dv = dot(jnp.concatenate(prob, axis=1), joint_g[p])
            return dsc, dk, dv

        for p in range(pairs):
            cols = slice(p * LANES, (p + 1) * LANES)
            queries += halves(q_ref[rows, cols] * 0.125)
            grads += halves(do_ref[rows, cols])
            joint_q.append(jnp.concatenate(queries[2 * p :], axis=0))
            joint_g.append(jnp.concatenate(grads[2 * p :], axis=0))
            prod = (do_ref[rows, cols].astype(F32) * o_ref[rows, cols].astype(F32)).T
            for h in range(2):
                inner.append(jnp.sum(prod[h * HEAD_DIM : (h + 1) * HEAD_DIM], axis=0, keepdims=True))
                sums.append(l_ref[0, 2 * p + h : 2 * p + h + 1, rows])
            keys = kp_ref[:, cols]
            dsc, dk, dv = pieces(keys, vp_ref[:, cols], p, None)
            if qb == 0:
                dkp_ref[:, cols] = dk
                dvp_ref[:, cols] = dv
            else:
                dkp_ref[:, cols] += dk
                dvp_ref[:, cols] += dv
            kpt = keys.T
            for h in range(2):
                carry.append(dot(kpt[h * HEAD_DIM : (h + 1) * HEAD_DIM], dsc[h]))

        def body(kb, carry):
            mask = key_mask(kb, (BLOCK, step), start, end)
            out = []
            at = pl.multiple_of(kb * BLOCK, BLOCK)
            for p in range(pairs):
                cols = slice(p * LANES, (p + 1) * LANES)
                keys = k_ref[pl.ds(at, BLOCK), cols]
                dsc, dk, dv = pieces(keys, v_ref[pl.ds(at, BLOCK), cols], p, mask)
                ka_ref[pl.ds(at, BLOCK), cols] += dk
                va_ref[pl.ds(at, BLOCK), cols] += dv
                kt = kt_ref[p, kb]
                for h in range(2):
                    out.append(
                        carry[2 * p + h] + dot(kt[h * HEAD_DIM : (h + 1) * HEAD_DIM], dsc[h])
                    )
            return tuple(out)

        carry = lax.fori_loop(lo_ref[qb], hi_ref[qb], body, tuple(carry))
        for p in range(pairs):
            both = jnp.concatenate(carry[2 * p : 2 * p + 2], axis=0)
            dq_ref[rows, p * LANES : (p + 1) * LANES] = (both.T * 0.125).astype(BF16)
    dk_ref[...] = ka_ref[...].astype(BF16)
    dv_ref[...] = va_ref[...].astype(BF16)


def specs(tokens, window, lanes, per):
    col = lambda i, *s: (0, i)
    return dict(
        tok=pl.BlockSpec((tokens, lanes), col),
        win=pl.BlockSpec((window, lanes), col),
        pre=pl.BlockSpec((PREFIX, lanes), col),
        bnd=pl.BlockSpec((8, tokens), lambda i, *s: (0, 0)),
        lse=pl.BlockSpec((1, per, tokens), lambda i, *s: (i, 0, 0)),
    )


def attend(lo, hi, q, k, v, kp, vp, bounds, lanes):
    tokens, width = q.shape
    window = k.shape[0]
    per = lanes // HEAD_DIM
    s = specs(tokens, window, lanes, per)
    return pl.pallas_call(
        attend_kernel,
        grid_spec=pltpu.PrefetchScalarGridSpec(
            num_scalar_prefetch=2,
            grid=(width // lanes,),
            in_specs=[s["tok"], s["win"], s["win"], s["pre"], s["pre"], s["bnd"]],
            out_specs=[s["tok"], s["lse"]],
            scratch_shapes=[pltpu.VMEM((lanes // LANES, window // BLOCK, LANES, BLOCK), BF16)],
        ),
        out_shape=[
            jax.ShapeDtypeStruct((tokens, width), BF16),
            jax.ShapeDtypeStruct((width // lanes, per, tokens), F32),
        ],
        name="attend",
    )(lo, hi, q, k, v, kp, vp, bounds)


def attend_back(lo, hi, q, k, v, kp, vp, bounds, o, lse, do, lanes):
    tokens, width = q.shape
    window = k.shape[0]
    s = specs(tokens, window, lanes, lanes // HEAD_DIM)
    return pl.pallas_call(
        attend_back_kernel,
        grid_spec=pltpu.PrefetchScalarGridSpec(
            num_scalar_prefetch=2,
            grid=(width // lanes,),
            in_specs=[
                s["tok"], s["win"], s["win"], s["pre"], s["pre"], s["bnd"],
                s["tok"], s["lse"], s["tok"],
            ],
            out_specs=[s["tok"], s["win"], s["win"], s["pre"], s["pre"]],
            scratch_shapes=[
                pltpu.VMEM((lanes // LANES, window // BLOCK, LANES, BLOCK), BF16),
                pltpu.VMEM((window, lanes), F32),
                pltpu.VMEM((window, lanes), F32),
            ],
        ),
        out_shape=[
            jax.ShapeDtypeStruct((tokens, width), BF16),
            jax.ShapeDtypeStruct((window, width), BF16),
            jax.ShapeDtypeStruct((window, width), BF16),
            jax.ShapeDtypeStruct((PREFIX, width), F32),
            jax.ShapeDtypeStruct((PREFIX, width), F32),
        ],
        name="attend_back",
    )(lo, hi, q, k, v, kp, vp, bounds, o, lse, do)


def up_kernel(x_ref, wu_ref, b_ref, wd_ref, acc_ref, slope_ref):
    e = dot(x_ref[...], wu_ref[...]) + b_ref[0:1, :]
    phi = 0.5 + 0.5 * lax.erf(e * 0.7071067811865476)
    slope_ref[...] = (phi + e * (0.3989422804014327 * jnp.exp(-0.5 * e * e))).astype(BF16)
    part = dot((e * phi).astype(BF16), wd_ref[...])

    @pl.when(pl.program_id(0) == 0)
    def _():
        acc_ref[...] = part

    @pl.when(pl.program_id(0) > 0)
    def _():
        acc_ref[...] += part


def down_kernel(g_ref, wd_ref, slope_ref, wu_ref, acc_ref):
    grad = dot_t(g_ref[...], wd_ref[...]) * slope_ref[...].astype(F32)
    part = dot_t(grad.astype(BF16), wu_ref[...])

    @pl.when(pl.program_id(0) == 0)
    def _():
        acc_ref[...] = part

    @pl.when(pl.program_id(0) > 0)
    def _():
        acc_ref[...] += part


def ffn_specs(tokens, width):
    return dict(
        act=pl.BlockSpec((tokens, width), lambda i: (0, 0)),
        up=pl.BlockSpec((width, FFBLOCK), lambda i: (0, i)),
        bias=pl.BlockSpec((1, FFBLOCK), lambda i: (0, i)),
        down=pl.BlockSpec((FFBLOCK, width), lambda i: (i, 0)),
        mid=pl.BlockSpec((tokens, FFBLOCK), lambda i: (0, i)),
    )


def ffn_up(x, wu, bias, wd):
    tokens, width = x.shape
    s = ffn_specs(tokens, width)
    return pl.pallas_call(
        up_kernel,
        grid=(wu.shape[1] // FFBLOCK,),
        in_specs=[s["act"], s["up"], s["bias"], s["down"]],
        out_specs=[s["act"], s["mid"]],
        out_shape=[
            jax.ShapeDtypeStruct((tokens, width), F32),
            jax.ShapeDtypeStruct((tokens, wu.shape[1]), BF16),
        ],
        name="ffn_up",
    )(x, wu, bias.reshape(1, -1), wd)


def ffn_down(g, wd, slope, wu):
    tokens, width = g.shape
    s = ffn_specs(tokens, width)
    return pl.pallas_call(
        down_kernel,
        grid=(wu.shape[1] // FFBLOCK,),
        in_specs=[s["act"], s["down"], s["mid"], s["up"]],
        out_specs=s["act"],
        out_shape=jax.ShapeDtypeStruct((tokens, width), F32),
        name="ffn_down",
    )(g, wd, slope, wu)


def swap(x, axis, bit, size):
    return lax.ppermute(x, axis, [(i, i ^ (1 << bit)) for i in range(size)])


def join(mine, theirs, axis, inner):
    count = mine.shape[axis] // inner
    parts = []
    for c in range(count):
        for side in (mine, theirs):
            parts.append(lax.slice_in_dim(side, c * inner, (c + 1) * inner, axis=axis))
    return jnp.concatenate(parts, axis=axis)


def bits_of(size):
    count = size.bit_length() - 1
    assert 1 << count == size
    return count


def gather(w, order, d_axis, rows, tp, done=()):
    block = w.shape[d_axis] >> len([o for o in done if o[0] == "rows"])
    have = set(bit for kind, bit in done if kind == "rows")
    for kind, bit in order[len(done) :]:
        if kind == "tp":
            w = join(w, swap(w, "tp", bit, tp), 1 - d_axis, w.shape[1 - d_axis])
        else:
            inner = w.shape[d_axis]
            if bit:
                inner = block * (1 << len([b for b in have if 0 < b < bit]))
            w = join(w, swap(w, "rows", bit, rows), d_axis, inner)
            have.add(bit)
    return w


def orders(rows, tp):
    zs = [("tp", b) for b in reversed(range(bits_of(tp)))]
    rs = [("rows", b) for b in range(1, bits_of(rows))]
    core = [("rows", 0)]
    half = len(rs) // 2
    return (
        zs[:-1] + rs + zs[-1:] + core,
        zs + rs + core,
        zs[:-1] + rs[half:] + zs[-1:] + rs[:half] + core,
    )


def reorder_kernel(at_ref, *refs):
    half = len(refs) // 2
    for a, b in zip(refs[:half], refs[half:]):
        b[...] = a[...]


def reorder(place, arrays):
    count = place.shape[0]
    width = arrays[0].shape[1]
    block = width // count
    if block % LANES:
        return [
            jnp.take(a.reshape(a.shape[0], count, block), place, axis=1).reshape(a.shape)
            for a in arrays
        ]
    return pl.pallas_call(
        reorder_kernel,
        grid_spec=pltpu.PrefetchScalarGridSpec(
            num_scalar_prefetch=1,
            grid=(count,),
            in_specs=[pl.BlockSpec((a.shape[0], block), lambda i, at: (0, at[i])) for a in arrays],
            out_specs=[pl.BlockSpec((a.shape[0], block), lambda i, at: (0, i)) for a in arrays],
        ),
        out_shape=[jax.ShapeDtypeStruct(a.shape, a.dtype) for a in arrays],
        name="reorder",
    )(place, *arrays)


def shift(x, step, tp):
    return lax.ppermute(x, "tp", [(i, i + step) for i in range(tp) if 0 <= i + step < tp])


def body(
    rows, tp,
    hidden, cotangent, pair_lengths, w_qkv, qkv_bias, w_out, w_up, up_bias, w_down,
    resid_bias, norm_gain, norm_bias, prefix_keys, prefix_values,
):
    tokens, row_count, width = hidden.shape
    assert row_count == 1
    local = w_qkv.shape[2]
    hops = -(-(MAXLEN - 1) // tokens)
    halo = hops * tokens
    window = tokens + 2 * halo
    lanes = min(width, 2 * LANES)
    here = lax.axis_index("tp")
    row = lax.axis_index("rows")
    order_a, order_b, order_c = orders(rows, tp)
    z_order = [o for o in order_b if o[0] == "tp"]
    nr = bits_of(rows)
    masks = [((s & ((rows >> 1) - 1)) << 1) | (s >> (nr - 1)) for s in range(rows)]
    place = (row ^ jnp.array(masks, jnp.int32)).astype(jnp.int32)

    hid, cot, shifts, gains, offsets = reorder(
        place, [hidden[:, 0], cotangent[:, 0], resid_bias, norm_gain, norm_bias]
    )
    shifts, gains, offsets = (a.astype(F32) for a in (shifts, gains, offsets))
    hid_window = jnp.concatenate(
        [shift(hid, j, tp) for j in range(hops, 0, -1)]
        + [hid]
        + [shift(hid, -j, tp) for j in range(1, hops + 1)],
        axis=0,
    )

    packed_small = jnp.concatenate(
        [prefix_keys, prefix_values, qkv_bias, up_bias.reshape(-1, local)], axis=0
    )
    small = gather(packed_small, z_order, 0, rows, tp)
    key_prefix, value_prefix = small[:PREFIX], small[PREFIX : 2 * PREFIX]
    biases = small[2 * PREFIX : 2 * PREFIX + 3].astype(F32)
    up_shift = (
        small[2 * PREFIX + 3 :].reshape(-1, tp, local).swapaxes(0, 1).reshape(-1).astype(F32)
    )

    early = min(EARLY, len(order_a) - 2)
    steps = (order_c, order_a, order_b)
    begun = [gather(w_qkv[i], steps[i][:early], 0, rows, tp) for i in range(3)]
    *begun, w_out, w_up, w_down = lax.optimization_barrier((*begun, w_out, w_up, w_down))
    wq, wk, wv = (
        gather(begun[i], steps[i], 0, rows, tp, steps[i][:early]) for i in range(3)
    )
    out_full = gather(w_out, order_c, 1, rows, tp)
    ff = w_up.shape[1] // 2
    up_full = [
        gather(w_up[:, :ff], order_a, 0, rows, tp),
        gather(w_up[:, ff:], order_b, 0, rows, tp),
    ]
    down_full = [
        gather(w_down[:ff], order_c, 1, rows, tp),
        gather(w_down[ff:], order_a, 1, rows, tp),
    ]
    up_shift = up_shift.reshape(tp, 2, ff)
    up_shifts = [up_shift[:, i].reshape(-1) for i in range(2)]

    ends = jnp.cumsum(pair_lengths[0])
    pad_id = ends.shape[0] - 1
    spot = here * tokens + jnp.arange(tokens, dtype=jnp.int32)
    past = spot[None, :] >= ends[:, None]
    seg = jnp.sum(past.astype(jnp.int32), axis=0)
    base = here * tokens - halo
    live = seg != pad_id
    first_key = jnp.max(jnp.where(past, ends[:, None], 0), axis=0) - base
    last_key = jnp.min(jnp.where(past, SEQ, ends[:, None]), axis=0) - base
    step = min(BLOCK, tokens)
    lo = jnp.min(jnp.where(live, first_key, window).reshape(-1, step), axis=1)
    hi = jnp.max(jnp.where(live, last_key, 0).reshape(-1, step), axis=1)
    lo = lo // BLOCK
    hi = jnp.maximum((hi + BLOCK - 1) // BLOCK, lo)
    zero = jnp.zeros_like(first_key)
    bounds = jnp.stack(
        [jnp.where(live, first_key, 0), jnp.where(live, last_key, 0)] + [zero] * 6, axis=0
    )

    q = (dot(hid, wq) + biases[0]).astype(BF16)
    k = (dot(hid_window, wk) + biases[1]).astype(BF16)
    v = (dot(hid_window, wv) + biases[2]).astype(BF16)
    mixed, lse = attend(lo, hi, q, k, v, key_prefix, value_prefix, bounds, lanes)
    first = hid.astype(F32) + dot(mixed, out_full) + shifts[0]
    normed = layer_norm(first, gains[0], offsets[0])
    normed_low = normed.astype(BF16)
    lifted = [ffn_up(normed_low, up_full[i], up_shifts[i], down_full[i]) for i in range(2)]
    second = normed + (lifted[0][0] + lifted[1][0]) + shifts[1]
    result = layer_norm(second, gains[1], offsets[1]).astype(BF16)

    grad_second = norm_back(second, gains[1], offsets[1], cot.astype(F32))
    grad_low = grad_second.astype(BF16)
    pushed = [ffn_down(grad_low, down_full[i], lifted[i][1], up_full[i]) for i in range(2)]
    grad_normed = grad_second + (pushed[0] + pushed[1])
    grad_first = norm_back(first, gains[0], offsets[0], grad_normed)
    grad_mixed = dot_t(grad_first.astype(BF16), out_full).astype(BF16)
    dq, dk, dv, dkp, dvp = attend_back(
        lo, hi, q, k, v, key_prefix, value_prefix, bounds, mixed, lse, grad_mixed, lanes
    )

    total = jnp.concatenate([dkp, dvp], axis=0)
    for kind, bit in reversed(z_order):
        half = total.shape[1] // 2
        sent = total[:, half:].astype(BF16)
        total = total[:, :half] + swap(sent, "tp", bit, tp).astype(F32)
    grad_kv = dot_t(dk, wk) + dot_t(dv, wv)
    sides = []
    for j in range(1, hops + 1):
        sides.append(grad_kv[halo - j * tokens : halo - (j - 1) * tokens].astype(BF16))
        sides.append(grad_kv[halo + j * tokens : halo + (j + 1) * tokens].astype(BF16))
    *sides, total = lax.optimization_barrier((*sides, total))
    grad_input = grad_kv[halo : halo + tokens] + dot_t(dq, wq) + grad_first
    for j in range(1, hops + 1):
        grad_input = grad_input + shift(sides[2 * j - 2], -j, tp).astype(F32)
        grad_input = grad_input + shift(sides[2 * j - 1], j, tp).astype(F32)
    for bit in range(nr):
        total = total + swap(total.astype(BF16), "rows", bit, rows).astype(F32)

    apart = (row ^ jnp.arange(rows, dtype=jnp.int32)).astype(jnp.int32)
    back = (apart >> 1) | ((apart & 1) << (nr - 1))
    result, grad_input = reorder(back, [result, grad_input])
    return result[:, None], grad_input[:, None], total[:PREFIX], total[PREFIX:]


def solution(mesh):
    placed = (
        P("tp", "rows", None),
        P("tp", "rows", None),
        P("rows", None),
        P(None, "rows", "tp"),
        P(None, "tp"),
        P("tp", "rows"),
        P("rows", "tp"),
        P("tp"),
        P("tp", "rows"),
        P(),
        P(),
        P(),
        P(None, "tp"),
        P(None, "tp"),
    )
    return jax.shard_map(
        partial(body, mesh.shape["rows"], mesh.shape["tp"]),
        mesh=mesh,
        in_specs=placed,
        out_specs=(P("tp", "rows", None), P("tp", "rows", None), P(None, "tp"), P(None, "tp")),
        check_vma=False,
    )
```
